32 devices in a mesh: sub: 8 (over z, x), load: 4 (over y, core).
Axes of the slice: x: 2, y: 2, z: 4, core: 2. Of those that a mesh axis runs over, the one named last changes fastest.
Arguments:
- dual_ops: bfloat16 [32, 1024, 1024], P(('sub', 'load')), may hold values from -0.1875 to 0.1875
- dual_rhs: float32 [32, 1024, 128], P(('sub', 'load')), may hold values from -6 to 6
- partner: int32 [32, 1024], P(('sub', 'load')), may hold values from 0 to 3071, as said below
- coarse_basis: bfloat16 [32, 12, 1024], P(('sub', 'load')), may hold values from -0.1875 to 0.1875
- coarse_inverse: float32 [384, 384], P(('sub', 'load')), as said below
- damping: float32 [128], replicated, may hold values from 0.05 to 0.5
- recovery: bfloat16 [32, 1536, 1024], P(('sub', 'load')), may hold values from -0.1875 to 0.1875
- base_disp: bfloat16 [32, 1536, 128], P(('sub', 'load')), may hold values from -6 to 6
- adjoint: bfloat16 [32, 1536, 128], P(('sub', 'load')), may hold values from -6 to 6
- elem_voxel: int32 [32, 128], P(('sub', 'load')), may hold values from 0 to 8191
- fibre_class: int32 [64, 512], P('sub', 'load'), may hold values from 0 to 3
Outputs:
- multipliers: float32 [32, 1024, 128], P(('sub', 'load'))
- gradient_field: float32 [64, 512], P('sub', 'load')
The draws below stay inside these ranges and needn't reach their ends.
Inputs may be any that keep to these rules, and one draw needn't show every extreme that they name: `partner`: entry (s, j) names the other copy of the same multiplier among the subdomains s - 1 (values 0 to 1023), s (1024 to 2047) and s + 1 (2048 to 3071), wrapping around over all 32 subdomains, as v mod 1024 = the copy's row. The pairing is one to one and symmetric; in every subdomain a quarter of the entries point to s - 1, a quarter to s + 1 and half inside. `elem_voxel`: value v places the element at grid row v // 128 and at column v mod 128 of the 128 columns of its subdomain's block of columns. coarse_inverse equals its transpose.
All inputs are finite; a program needn't handle non-finite values.
Results may differ from the reference program's by a relative error of at most 0.0021.
Values may be sent and summed in bfloat16 or wider, within the bound.
A program may use at most 64 MiB of HBM per device.

```python
import math
import jax
import jax.numpy as jnp
import numpy as np
from jax import lax

M = 1024
C = 128
U = 1536
R = 12
EDOF = 12
ITERS = 3
SMOOTH = 2
VY = 128
SUBS = 32
NCOARSE = 384
NE = 128
GX = 64
GY = 512


def draw_partner(key, part):
    quarter = M // 4
    row_keys = jax.random.split(key, SUBS)
    orders = jax.vmap(lambda single_key: jax.random.permutation(single_key, M))(row_keys).astype(jnp.int32)
    following = jnp.roll(orders, -1, axis=0)
    preceding = jnp.roll(orders, 1, axis=0)
    inner = orders[:, 2 * quarter:].reshape(SUBS, -1, 2)[:, :, ::-1].reshape(SUBS, -1)
    targets = jnp.concatenate([2 * M + following[:, quarter:2 * quarter], preceding[:, :quarter], M + inner], axis=1)
    owner_ids = lax.broadcasted_iota(jnp.int32, orders.shape, 0)
    placed = jnp.zeros(orders.shape, jnp.int32).at[owner_ids, orders].set(targets)
    return placed


def draw_coarse_inverse(key, part):
    raw = jnp.clip(jax.random.normal(jax.random.fold_in(key, 17), (NCOARSE, NCOARSE), jnp.float32), -6.0, 6.0)
    return (raw + raw.T) / jnp.sqrt(2.0 * NCOARSE)


def place_ends(entries, key, least, high):
    dims = entries.shape
    place = [jax.random.randint(jax.random.fold_in(key, axis), (), 0, dims[axis]) for axis in range(len(dims))]
    entries = entries.at[tuple(place)].set(least)
    longest = dims.index(max(dims))
    place[longest] = (place[longest] + 1) % dims[longest]
    return entries.at[tuple(place)].set(high)


def block_scale(own_key, shape, pieces, smallest, top_value):
    level = 1.0
    for axis_at, parts in pieces:
        heights = jax.random.uniform(jax.random.fold_in(jax.random.fold_in(own_key, 6), axis_at), (parts,), jnp.float32, smallest / len(pieces), top_value / len(pieces))
        level = level * jnp.repeat(jnp.exp(heights), shape[axis_at] // parts).reshape((-1,) + (1,) * (len(shape) - 1 - axis_at))
    return level


def rank_table(amount, slope):
    portions = [(1 << 20) // math.isqrt(rank ** slope) + 1 for rank in range(1, amount + 1)]
    scale = 1 + sum(portions) // (1 << 30)
    return np.cumsum(np.array([max(1, weight // scale) for weight in portions]))


def ranked(key, dims, count, skew):
    table = rank_table(count, skew)
    lot = jax.random.randint(jax.random.fold_in(key, 1), dims, 0, int(table[count - 1]))
    standing = jnp.searchsorted(jnp.asarray(table, jnp.int32), lot, side="right")
    return jax.random.permutation(jax.random.fold_in(key, 2), count)[standing].astype(jnp.int32)


def bell_draw(rng, shape, spread, limit, shards=(), held_as=jnp.bfloat16):
    level = block_scale(rng, shape, shards, -0.22, 0.18) if shards else 1.0
    values = jax.random.normal(rng, shape, jnp.float32) * spread * level
    return jnp.minimum(jnp.maximum(values, -limit), limit).astype(held_as)


def setup_inputs(seed: int = 0) -> dict:
    splits = jax.random.split(jax.random.key(seed), 12)
    return {
        "dual_ops": bell_draw(splits[0], (SUBS, M, M), M ** -0.5, 0.1875, ((0, 32),)),
        "dual_rhs": bell_draw(splits[1], (SUBS, M, C), 1.0, 6.0, ((0, 32),), jnp.float32),
        "partner": draw_partner(jax.random.fold_in(splits[11], 71), 0),
        "coarse_basis": bell_draw(splits[3], (SUBS, R, M), M ** -0.5, 0.1875, ((0, 32),)),
        "coarse_inverse": draw_coarse_inverse(jax.random.fold_in(splits[11], 71), 0),
        "damping": jnp.clip(jnp.exp(jax.random.uniform(splits[5], (C,), jnp.float32, math.log(0.05), math.log(0.5))), 0.05, 0.5),
        "recovery": bell_draw(splits[6], (SUBS, U, M), M ** -0.5, 0.1875, ((0, 32),)),
        "base_disp": bell_draw(splits[7], (SUBS, U, C), 1.0, 6.0, ((0, 32),)),
        "adjoint": bell_draw(splits[8], (SUBS, U, C), 1.0, 6.0, ((0, 32),)),
        "elem_voxel": place_ends(ranked(splits[9], (SUBS, NE), GX * VY, 2), jax.random.fold_in(splits[9], 3), 0, (GX * VY) - 1).astype(jnp.int32),
        "fibre_class": place_ends(jax.random.randint(splits[10], (GX, GY), 0, 4), jax.random.fold_in(splits[10], 1), 0, 3).astype(jnp.int32),
    }


FIBRE_RATE = 0.3
ISO_RATE = 0.05
EPSILON = 1e-06

def apply_all(matrices, values):

    def single(operands):
        return jnp.dot(operands[0], operands[1], preferred_element_type=jnp.float32)
    return lax.map(single, (matrices, values))

def partner_index(partner):
    slot_rows = lax.broadcasted_iota(jnp.int32, (SUBS, M), 0)
    window_side = partner // M
    neighbour = (slot_rows + window_side - 1 + SUBS) % SUBS
    return (neighbour * M + partner % M).astype(jnp.int32).reshape(-1)

def fibre_step(smoothed, classes):
    padded = jnp.pad(smoothed, 1)
    along_rows = padded[2:, 1:-1] + padded[:-2, 1:-1] - 2.0 * smoothed
    along_cols = padded[1:-1, 2:] + padded[1:-1, :-2] - 2.0 * smoothed
    diag_main = padded[2:, 2:] + padded[:-2, :-2] - 2.0 * smoothed
    diag_anti = padded[2:, :-2] + padded[:-2, 2:] - 2.0 * smoothed
    chosen = jnp.where(classes == 0, along_rows, jnp.where(classes == 1, along_cols, jnp.where(classes == 2, diag_main, diag_anti)))
    return smoothed + FIBRE_RATE * chosen + ISO_RATE * (along_rows + along_cols)

def reference(dual_ops, dual_rhs, partner, coarse_basis, coarse_inverse, damping, recovery, base_disp, adjoint, elem_voxel, fibre_class):
    mode_basis = coarse_basis.astype(jnp.float32)
    flat_index = partner_index(partner)
    dual_iterate = jnp.zeros((SUBS, M, C), jnp.float32)
    for iteration in range(ITERS):
        images = apply_all(dual_ops, dual_iterate.astype(jnp.bfloat16)).astype(jnp.bfloat16)
        partners = jnp.take(images.reshape(SUBS * M, C), flat_index, axis=0).reshape(SUBS, M, C)
        residual = dual_rhs - (images.astype(jnp.float32) + partners.astype(jnp.float32))
        coarse_terms = jnp.einsum('sqj,sjc->sqc', mode_basis, residual, precision=lax.Precision.HIGHEST).reshape(SUBS * R, C)
        squares = lax.optimization_barrier(jnp.sum(residual * residual, axis=(0, 1)))
        correction = jnp.dot(coarse_inverse, coarse_terms, precision=lax.Precision.HIGHEST)
        step_size = damping / jnp.sqrt(squares / (SUBS * M) + EPSILON)
        projected = residual - jnp.einsum('sqj,sqc->sjc', mode_basis, correction.reshape(SUBS, R, C), precision=lax.Precision.HIGHEST)
        dual_iterate = dual_iterate + step_size[None, None, :] * projected
    multipliers = dual_iterate
    displaced = base_disp.astype(jnp.float32) - apply_all(recovery, multipliers.astype(jnp.bfloat16))
    products = (displaced * adjoint.astype(jnp.float32)).reshape(SUBS, NE, EDOF, C)
    element_grad = lax.optimization_barrier(jnp.sum(products, axis=(2, 3))) / math.sqrt(EDOF * C)
    subdomain_ids = lax.broadcasted_iota(jnp.int32, (SUBS, NE), 0)
    column_block = subdomain_ids % (GY // VY)
    grid_index = elem_voxel // VY * GY + column_block * VY + elem_voxel % VY
    smoothed = jax.ops.segment_sum(element_grad.reshape(-1), grid_index.reshape(-1).astype(jnp.int32), num_segments=GX * GY).reshape(GX, GY)
    for repeat in range(SMOOTH):
        smoothed = fibre_step(smoothed, fibre_class)
    return (multipliers, smoothed)
```

```python
import functools
import math

import jax
import jax.numpy as jnp
from jax import lax
from jax.experimental import pallas as pl
from jax.experimental.pallas import tpu as pltpu
from jax.sharding import PartitionSpec as P

EDOF = 12
ITERS = 3
SMOOTH = 2
FIBRE_RATE = 0.3
ISO_RATE = 0.05
EPSILON = 1e-06

F32 = jnp.float32
BF16 = jnp.bfloat16
I32 = jnp.int32
MESH = pl.DeviceIdType.MESH
LANES = 128
CHUNK = 256
RP = 16
GROUP = 32
MARGIN_R = 4
MARGIN_C = 64


def iota(shape, dim):
    return lax.broadcasted_iota(I32, shape, dim)


def hot(cond):
    return jnp.where(cond, 1.0, 0.0).astype(BF16)


def split(value):
    high = value.astype(BF16)
    return high, (value - high.astype(F32)).astype(BF16)


def kernel(
    ns, nl,
    a_h, rhs_h, par_h, b_h, ci_h, damp_h, rec_h, base_h, adj_h, ev_h, fc_h,
    x_h, f_h,
    a, rhs, par, b, ci, damp, rec, base, adj, evb, fcb,
    own_hot, recv_hot, send_hot, x, xr, img, y, res, parts, snd, rcv, snd1, rcv1,
    bwide, bt, bp, spread, cpf, cp, ag, ck, hw, ckw, rb, da, db,
    prod, sel, egb, colhot, rowval, fout,
    lsem, nsend, nrecv, gsend, grecv, psend, precv, vsend, vrecv, csend, crecv, esend, erecv,
):
    n = ns * nl
    spots = a.shape[0]
    quarter = spots // 4
    modes = b.shape[0]
    sub, load = lax.axis_index("sub"), lax.axis_index("load")
    me = sub * nl + load

    def dev(p):
        return (lax.div(p, nl), lax.rem(p, nl))

    def peer(k):
        return lax.rem(me + k, n)

    local = [
        pltpu.make_async_copy(src, dst, lsem.at[i])
        for i, (src, dst) in enumerate((
            (b_h.at[0], b),
            (rhs_h.at[0], rhs),
            (par_h, par),
            (ci_h, ci),
            (damp_h, damp),
            (a_h.at[0], a),
            (ev_h, evb.at[me]),
            (fc_h, fcb.at[4]),
            (rec_h.at[0], rec),
            (base_h.at[0], base),
            (adj_h.at[0], adj),
        ))
    ]
    for copy in local[:8]:
        copy.start()

    barrier = pltpu.get_barrier_semaphore()

    def each_peer(act):
        @pl.loop(0, ns)
        def _(i):
            far = jnp.where(2 * sub < ns, ns - 1 - i, i)
            for j in range(nl):
                across = jnp.where(2 * load < nl, nl - 1 - j, j)

                @pl.when(far * nl + across != me)
                def _():
                    act((far, across))

    each_peer(lambda to: pl.semaphore_signal(barrier, inc=1, device_id=to, device_id_type=MESH))

    def to_all(ref, send, recv):
        each_peer(lambda to: pltpu.make_async_remote_copy(
            src_ref=ref.at[me], dst_ref=ref.at[me], send_sem=send, recv_sem=recv,
            device_id=to, device_id_type=MESH,
        ).start())

    def settle(ref, sem):
        part = ref.at[pl.ds(0, n - 1)]
        pltpu.make_async_copy(part, part, sem).wait()

    def chunk(r):
        return pl.ds(r * CHUNK, CHUNK)

    chunks = spots // CHUNK

    def gather_terms(it, total):
        both = jnp.dot(bp[...], parts[...], preferred_element_type=F32)
        terms = both[:, 0:LANES] + both[:, LANES:2 * LANES]
        squares = jnp.sum(total, axis=0, keepdims=True)
        high, rest = split(squares)
        row = iota((RP, LANES), 0)
        terms = jnp.where(row == modes, high.astype(F32), terms)
        terms = jnp.where(row == modes + 1, rest.astype(F32), terms)
        ag[it, me] = terms.astype(BF16)

    def keep_parts(rows, left):
        high, rest = split(left)
        parts[rows, 0:LANES] = high
        parts[rows, LANES:2 * LANES] = rest
        return jnp.sum((left * left).reshape(CHUNK // 8, 8, LANES), axis=0)

    blocks = spots // LANES
    local[0].wait()
    bwide[...] = jnp.zeros_like(bwide)
    basis = b[...].astype(F32)
    for d in range(4):
        bwide[d * RP:d * RP + modes, :] = basis
    bp[...] = bwide[0:RP, :].astype(BF16)
    local[1].wait()
    total = jnp.zeros((8, LANES), F32)
    for r in range(chunks):
        total = total + keep_parts(chunk(r), rhs[chunk(r), :])
    gather_terms(0, total)

    for r in range(blocks):
        bt[pl.ds(r * LANES, LANES), :] = jnp.transpose(
            bwide[:, r * LANES:(r + 1) * LANES]
        ).astype(BF16)
    ck[...] = jnp.zeros_like(ck)
    ckw[...] = jnp.zeros_like(ckw)
    local[3].wait()
    deep, broad = spread.shape
    at_col = iota((deep, broad), 1)
    within = at_col & (RP - 1)
    from_row = (at_col >> 4) * modes + within
    spread[...] = hot((iota((deep, broad), 0) == from_row) & (within < modes))
    cpf[...] = jnp.zeros_like(cpf)
    for g in range(n // GROUP):
        high, rest = split(ci[:, g * deep:(g + 1) * deep])
        cols = pl.ds(g * broad, broad)
        cpf[0:modes, cols] = jnp.dot(high, spread[...], preferred_element_type=F32)
        cpf[RP:RP + modes, cols] = jnp.dot(rest, spread[...], preferred_element_type=F32)
        mode = iota((1, broad), 1) & (RP - 1)
        cpf[modes:modes + 1, cols] = jnp.where((mode == modes) | (mode == modes + 1), 1.0, 0.0)
    own_cp = pl.ds(4 * RP, 2 * RP)
    cp[own_cp, :] = cpf[...].astype(BF16)

    local[2].wait()
    prow = par[...].astype(F32)
    to_next = jnp.where(prow >= float(2 * spots), 1.0, 0.0)
    to_prev = jnp.where(prow < float(spots), 1.0, 0.0)
    count = jnp.where(iota((8, spots), 0) == 0, to_next, to_prev)
    wide = iota((8, spots), 1)
    shift = 1
    while shift < spots:
        count = count + jnp.where(wide >= shift, pltpu.roll(count, shift, 1), 0.0)
        shift *= 2
    slot = jnp.where(
        to_next > 0.5,
        count[0:1] - 1.0,
        jnp.where(to_prev > 0.5, count[1:2] - 1.0 + float(quarter), -1.0),
    )
    for r in range(2 * quarter // LANES):
        at = (iota((LANES, spots), 0) + r * LANES).astype(F32)
        send_hot[pl.ds(r * LANES, LANES), :] = hot(slot == at)

    for i in (4, 5, 6, 7):
        local[i].wait()
    for copy in local[8:]:
        copy.start()

    pl.semaphore_wait(barrier, n - 1)
    to_all(ag.at[0], gsend.at[0], grecv.at[0])
    near = []
    for side, step in enumerate((1, n - 1)):
        copy = pltpu.make_async_remote_copy(
            src_ref=cp.at[own_cp], dst_ref=cp.at[pl.ds(side * 2 * RP, 2 * RP)],
            send_sem=psend.at[side], recv_sem=precv.at[side],
            device_id=dev(peer(step)), device_id_type=MESH,
        )
        copy.start()
        near.append(copy)

    def exchange(it):
        copies = []
        for side, step in enumerate((1, n - 1)):
            half = pl.ds(side * quarter, quarter)
            src, dst = (snd, rcv) if it == 0 else (snd1, rcv1)
            copy = pltpu.make_async_remote_copy(
                src_ref=src.at[half], dst_ref=dst.at[half],
                send_sem=nsend.at[it, side], recv_sem=nrecv.at[it, side],
                device_id=dev(peer(step)), device_id_type=MESH,
            )
            copy.start()
            copies.append(copy)
        return copies

    for r in range(chunks):
        rows = chunk(r)
        xr[rows, 0:LANES] = parts[rows, 0:LANES]
        xr[rows, LANES:2 * LANES] = bt[rows, :]
    first_modes = iota((CHUNK, LANES), 1) < RP
    for r in range(chunks):
        rows = chunk(r)
        out = jnp.dot(a[rows, :], xr[...], preferred_element_type=F32)
        img[rows, 0:LANES] = out[:, 0:LANES].astype(BF16)
        g = out[:, LANES:2 * LANES]
        y[rows, :] = g
        high, rest = split(g)
        img[rows, LANES:2 * LANES] = jnp.where(first_modes, high.astype(F32), rest.astype(F32)).astype(BF16)
    snd[...] = jnp.dot(send_hot[...], img[...], preferred_element_type=F32).astype(BF16)
    pair = exchange(0)

    to_all(evb, vsend, vrecv)
    around = [(i, j) for i in (-1, 0, 1) for j in (-1, 0, 1) if (i, j) != (0, 0)]
    for i, j in around:
        pltpu.make_async_remote_copy(
            src_ref=fcb.at[4], dst_ref=fcb.at[(1 - i) * 3 + 1 - j],
            send_sem=csend, recv_sem=crecv,
            device_id=(lax.rem(sub + i + ns, ns), lax.rem(load + j + nl, nl)),
            device_id_type=MESH,
        ).start()

    lane = iota((LANES, LANES), 1).astype(F32)
    for r in range(blocks):
        rows = pl.ds(r * LANES, LANES)
        pcol = jnp.transpose(jnp.broadcast_to(prow[:, r * LANES:(r + 1) * LANES], (LANES, LANES)))
        below = jnp.zeros((LANES, LANES), F32)
        for c in range(blocks):
            cols = pl.ds(c * LANES, LANES)
            own_hot[rows, cols] = hot(pcol == lane + float(spots + c * LANES))
            below = below + jnp.where(pcol > prow[:, c * LANES:(c + 1) * LANES], 1.0, 0.0)
        rank = jnp.broadcast_to(jnp.sum(below, axis=1, keepdims=True), (LANES, LANES))
        place = jnp.where(
            pcol < float(spots),
            rank,
            jnp.where(pcol >= float(2 * spots), rank - float(2 * quarter), -1.0),
        )
        for c in range(2 * quarter // LANES):
            recv_hot[rows, pl.ds(c * LANES, LANES)] = hot(place == lane + float(c * LANES))
    offset = iota(sel.shape, 1) - EDOF * iota(sel.shape, 0)
    sel[...] = hot((offset >= 0) & (offset < EDOF))

    block_at = iota((CHUNK, LANES), 1) >> 4
    for r in range(chunks):
        rows = chunk(r)
        mine = jnp.dot(own_hot[rows, :], img[...], preferred_element_type=F32)
        inner = mine[:, LANES:2 * LANES]
        inner = inner + pltpu.roll(inner, LANES - RP, 1)
        inner = jnp.where(first_modes, inner, 0.0)
        inner = inner + pltpu.roll(inner, RP, 1)
        g = y[rows, :] + inner
        high, rest = split(g)
        g = jnp.where(first_modes, high.astype(F32), rest.astype(F32))
        g = jnp.where(block_at < 2, g, 0.0)
        da[rows, :] = pltpu.roll(g, 4 * RP, 1)
        y[rows, :] = img[rows, 0:LANES].astype(F32) + mine[:, 0:LANES]

    for copy in pair:
        copy.wait_recv()
    upper = pl.ds(quarter, quarter)
    wide_lane = iota((quarter, LANES), 1)
    moved_part = jnp.where(wide_lane < 2 * RP, rcv[upper, LANES:2 * LANES].astype(F32), 0.0)
    rcv[upper, LANES:2 * LANES] = pltpu.roll(moved_part, 2 * RP, 1).astype(BF16)
    lower = pl.ds(0, quarter)
    rcv[lower, LANES:2 * LANES] = jnp.where(
        wide_lane < 2 * RP, rcv[lower, LANES:2 * LANES].astype(F32), 0.0
    ).astype(BF16)
    for r in range(chunks):
        rows = chunk(r)
        other = jnp.dot(recv_hot[rows, :], rcv[...], preferred_element_type=F32)
        y[rows, :] = y[rows, :] + other[:, 0:LANES]
        modes_image = (da[rows, :] + other[:, LANES:2 * LANES]).astype(BF16)
        hw[rows, 0:LANES] = modes_image
        hw[rows, LANES:2 * LANES] = modes_image

    entries = float(n * spots)

    def solve(it):
        settle(ag.at[it], grecv.at[it])
        solved = jnp.dot(
            cp[...], ag[it].reshape(n * RP, LANES), preferred_element_type=F32
        )
        cs = [solved[2 * d * RP:(2 * d + 1) * RP] + solved[(2 * d + 1) * RP:(2 * d + 2) * RP] for d in range(3)]
        mean = cs[2][modes:modes + 1] / entries
        step_size = damp[...] / jnp.sqrt(mean + EPSILON)
        return cs, step_size

    def advance(step_size, before, first):
        for r in range(chunks):
            rows = chunk(r)
            move = step_size * (before[rows, :] - jnp.dot(bt[rows, :], ck[...], preferred_element_type=F32))
            x[rows, :] = move if first else x[rows, :] + move

    for it in range(ITERS - 1):
        before = rhs if it == 0 else res.at[it - 1]
        if it == 0:
            for copy in near:
                copy.wait_recv()
        cs, step_size = solve(it)
        for d in range(3):
            high, rest = split(cs[d])
            for k in range(2):
                ckw[(2 * d + k) * RP:(2 * d + k + 1) * RP, :] = high
                ckw[LANES + (2 * d + k) * RP:LANES + (2 * d + k + 1) * RP, :] = rest
            if d == 2:
                ck[0:RP, :] = high
                ck[RP:2 * RP, :] = rest
        total = jnp.zeros((8, LANES), F32)
        for r in range(chunks):
            rows = chunk(r)
            left = before[rows, :] - step_size * (
                y[rows, :] - jnp.dot(hw[rows, :], ckw[...], preferred_element_type=F32)
            )
            res[it, rows, :] = left
            total = total + keep_parts(rows, left)
        gather_terms(it + 1, total)
        to_all(ag.at[it + 1], gsend.at[it + 1], grecv.at[it + 1])

        if it + 2 < ITERS:
            for r in range(chunks):
                rows = chunk(r)
                img[rows, 0:LANES] = jnp.dot(
                    a[rows, :], parts[:, 0:LANES], preferred_element_type=F32
                ).astype(BF16)
            snd1[...] = jnp.dot(
                send_hot[...], img[:, 0:LANES], preferred_element_type=F32
            ).astype(BF16)
            near = near + pair
            pair = exchange(it + 1)
            advance(step_size, before, it == 0)
            for r in range(chunks):
                rows = chunk(r)
                y[rows, :] = img[rows, 0:LANES].astype(F32) + jnp.dot(
                    own_hot[rows, :], img[:, 0:LANES], preferred_element_type=F32
                )
            if it == 0:
                settle(evb, vrecv)

                @pl.loop(0, n)
                def _(s):
                    column = evb[s] & (LANES - 1)
                    spot = (lax.rem(s, nl) - load) * LANES + column + MARGIN_C
                    colhot[:, pl.ds(pl.multiple_of(s * LANES, LANES), LANES)] = hot(
                        iota((2 * LANES, LANES), 0) == spot
                    )
            for copy in pair:
                copy.wait_recv()
            for r in range(chunks):
                rows = chunk(r)
                y[rows, :] = y[rows, :] + jnp.dot(
                    recv_hot[rows, :], rcv1[...], preferred_element_type=F32
                )
        else:
            advance(step_size, before, it == 0)

    last = res.at[ITERS - 2]
    for r in range(chunks):
        rows = chunk(r)
        xr[rows, 0:LANES] = x[rows, :].astype(BF16)
        xr[rows, LANES:2 * LANES] = parts[rows, 0:LANES]
    for copy in local[8:]:
        copy.wait()
    unknowns = rec.shape[0]
    for r in range(unknowns // CHUNK):
        rows = chunk(r)
        out = jnp.dot(rec[rows, :], xr[...], preferred_element_type=F32)
        da[rows, :] = base[rows, :].astype(F32) - out[:, 0:LANES]
        db[rows, :] = out[:, LANES:2 * LANES]
        g = jnp.dot(rec[rows, :], bt[...], preferred_element_type=F32)
        high, rest = split(g)
        rb[rows, :] = jnp.where((block_at & 1) == 0, high.astype(F32), rest.astype(F32)).astype(BF16)

    cs, step_size = solve(ITERS - 1)
    high, rest = split(cs[2])
    ck[0:RP, :] = high
    ck[RP:2 * RP, :] = rest
    ckw[0:RP, :] = high
    ckw[RP:2 * RP, :] = high
    ckw[2 * RP:3 * RP, :] = rest
    ckw[3 * RP:4 * RP, :] = rest
    for r in range(unknowns // CHUNK):
        rows = chunk(r)
        displaced = da[rows, :] - step_size * (
            db[rows, :] - jnp.dot(rb[rows, 0:4 * RP], ckw[0:4 * RP, :], preferred_element_type=F32)
        )
        high, rest = split(displaced * adj[rows, :].astype(F32))
        prod[rows, 0:LANES] = high
        prod[rows, LANES:2 * LANES] = rest

    both = jnp.dot(sel[...], prod[...], preferred_element_type=F32)
    grads = jnp.sum(
        jnp.transpose(both[:, 0:LANES] + both[:, LANES:2 * LANES]), axis=0, keepdims=True
    ) / math.sqrt(EDOF * LANES)
    egb[me] = grads
    to_all(egb, esend, erecv)

    advance(step_size, last, False)
    out_copy = pltpu.make_async_copy(x, x_h.at[0], lsem.at[11])
    out_copy.start()

    pltpu.make_async_copy(fcb.at[pl.ds(0, 8)], fcb.at[pl.ds(0, 8)], crecv).wait()
    classes = jnp.concatenate(
        [jnp.concatenate([fcb[3 * i + j] for j in range(3)], axis=1) for i in range(3)], axis=0
    )
    high_r, wide_c = 2 * 8, 2 * LANES
    classes = pltpu.roll(classes, 3 * 8 - (8 - MARGIN_R), 0)[0:high_r]
    classes = pltpu.roll(classes, 3 * LANES - (LANES - MARGIN_C), 1)[:, 0:wide_c]
    grid_row = iota((high_r, wide_c), 0) + (sub * 8 - MARGIN_R)
    grid_col = iota((high_r, wide_c), 1) + (load * LANES - MARGIN_C)
    inside = (grid_row >= 0) & (grid_row < ns * 8) & (grid_col >= 0) & (grid_col < nl * LANES)

    settle(egb, erecv)

    def place_rows(s, carry):
        here = iota((RP, LANES), 0) == (evb[s] >> 7) - (sub * 8 - MARGIN_R)
        high, rest = split(jnp.where(here, egb[s], 0.0))
        cols = pl.ds(pl.multiple_of(s * LANES, LANES), LANES)
        rowval[0:RP, cols] = high
        rowval[RP:2 * RP, cols] = rest
        return carry

    lax.fori_loop(0, n, place_rows, 0, unroll=8)
    sums = lax.dot_general(
        rowval[...], colhot[...], (((1,), (1,)), ((), ())), preferred_element_type=F32
    )
    field = sums[0:RP] + sums[RP:2 * RP]

    def moved(value, by_row, by_col):
        if by_row:
            value = pltpu.roll(value, (-by_row) % high_r, 0)
        if by_col:
            value = pltpu.roll(value, (-by_col) % wide_c, 1)
        return value

    for repeat in range(SMOOTH):
        field = jnp.where(inside, field, 0.0)
        up, down = moved(field, 1, 0), moved(field, -1, 0)
        along_rows = up + down - 2.0 * field
        along_cols = moved(field, 0, 1) + moved(field, 0, -1) - 2.0 * field
        diag_main = moved(up, 0, 1) + moved(down, 0, -1) - 2.0 * field
        diag_anti = moved(up, 0, -1) + moved(down, 0, 1) - 2.0 * field
        chosen = jnp.where(
            classes == 0,
            along_rows,
            jnp.where(classes == 1, along_cols, jnp.where(classes == 2, diag_main, diag_anti)),
        )
        field = field + FIBRE_RATE * chosen + ISO_RATE * (along_rows + along_cols)
    fout[...] = moved(field, MARGIN_R, MARGIN_C)[0:8, 0:LANES]
    field_copy = pltpu.make_async_copy(fout, f_h, lsem.at[12])
    field_copy.start()

    for copy in near + pair:
        copy.wait_send()
    for it in range(ITERS):
        settle(ag.at[it], gsend.at[it])
    settle(evb, vsend)
    settle(egb, esend)
    pltpu.make_async_copy(fcb.at[pl.ds(0, 8)], fcb.at[pl.ds(0, 8)], csend).wait()
    out_copy.wait()
    field_copy.wait()


def on_device(ns, nl, *args):
    (dual_ops, dual_rhs, partner, coarse_basis, coarse_inverse, damping,
     recovery, base_disp, adjoint, elem_voxel, fibre_class) = args
    n = ns * nl
    spots, columns = dual_rhs.shape[1:]
    modes = coarse_basis.shape[1]
    unknowns = recovery.shape[1]
    elements = elem_voxel.shape[1]
    half = spots // 2
    dma = pltpu.SemaphoreType.DMA
    scratch = [
        pltpu.VMEM((spots, spots), BF16),
        pltpu.VMEM((spots, columns), F32),
        pltpu.VMEM((1, spots), I32),
        pltpu.VMEM((modes, spots), BF16),
        pltpu.VMEM(coarse_inverse.shape, F32),
        pltpu.VMEM((1, columns), F32),
        pltpu.VMEM((unknowns, spots), BF16),
        pltpu.VMEM((unknowns, columns), BF16),
        pltpu.VMEM((unknowns, columns), BF16),
        pltpu.VMEM((n, 1, elements), I32),
        pltpu.VMEM((9,) + fibre_class.shape, I32),
        pltpu.VMEM((spots, spots), BF16),
        pltpu.VMEM((spots, half), BF16),
        pltpu.VMEM((half, spots), BF16),
        pltpu.VMEM((spots, columns), F32),
        pltpu.VMEM((spots, 2 * columns), BF16),
        pltpu.VMEM((spots, 2 * columns), BF16),
        pltpu.VMEM((spots, columns), F32),
        pltpu.VMEM((ITERS - 1, spots, columns), F32),
        pltpu.VMEM((spots, 2 * columns), BF16),
        pltpu.VMEM((half, 2 * columns), BF16),
        pltpu.VMEM((half, 2 * columns), BF16),
        pltpu.VMEM((half, columns), BF16),
        pltpu.VMEM((half, columns), BF16),
        pltpu.VMEM((LANES, spots), F32),
        pltpu.VMEM((spots, LANES), BF16),
        pltpu.VMEM((RP, spots), BF16),
        pltpu.VMEM((GROUP * modes, GROUP * RP), BF16),
        pltpu.VMEM((2 * RP, n * RP), F32),
        pltpu.VMEM((6 * RP, n * RP), BF16),
        pltpu.VMEM((ITERS, n, RP, columns), BF16),
        pltpu.VMEM((LANES, columns), BF16),
        pltpu.VMEM((spots, 2 * LANES), BF16),
        pltpu.VMEM((2 * LANES, columns), BF16),
        pltpu.VMEM((unknowns, LANES), BF16),
        pltpu.VMEM((unknowns, columns), F32),
        pltpu.VMEM((unknowns, columns), F32),
        pltpu.VMEM((unknowns, 2 * columns), BF16),
        pltpu.VMEM((elements, unknowns), BF16),
        pltpu.VMEM((n, 1, elements), F32),
        pltpu.VMEM((2 * LANES, n * elements), BF16),
        pltpu.VMEM((2 * RP, n * elements), BF16),
        pltpu.VMEM(fibre_class.shape, F32),
        dma((13,)),
        dma((ITERS - 1, 2)),
        dma((ITERS - 1, 2)),
        dma((ITERS,)),
        dma((ITERS,)),
        dma((2,)),
        dma((2,)),
        dma, dma, dma, dma, dma, dma,
    ]
    anywhere = pl.BlockSpec(memory_space=pl.ANY)
    multipliers, field = pl.pallas_call(
        functools.partial(kernel, ns, nl),
        out_shape=(
            jax.ShapeDtypeStruct((1, spots, columns), F32),
            jax.ShapeDtypeStruct(fibre_class.shape, F32),
        ),
        in_specs=[anywhere] * 11,
        out_specs=(anywhere, anywhere),
        scratch_shapes=scratch,
        compiler_params=pltpu.CompilerParams(
            collective_id=0, has_side_effects=True, vmem_limit_bytes=62 * 1024 * 1024
        ),
    )(
        dual_ops, dual_rhs, partner, coarse_basis, coarse_inverse,
        damping.reshape(1, columns), recovery, base_disp, adjoint, elem_voxel, fibre_class,
    )
    return multipliers, field


def solution(mesh):
    ns, nl = mesh.shape["sub"], mesh.shape["load"]
    placed = (
        P(("sub", "load"), None, None),
        P(("sub", "load"), None, None),
        P(("sub", "load"), None),
        P(("sub", "load"), None, None),
        P(("sub", "load"), None),
        P(),
        P(("sub", "load"), None, None),
        P(("sub", "load"), None, None),
        P(("sub", "load"), None, None),
        P(("sub", "load"), None),
        P("sub", "load"),
    )
    return jax.shard_map(
        functools.partial(on_device, ns, nl),
        mesh=mesh,
        in_specs=placed,
        out_specs=(P(("sub", "load"), None, None), P("sub", "load")),
        check_vma=False,
    )
```

```python
import functools
import math

import jax
import jax.numpy as jnp
from jax import lax
from jax.experimental import pallas as pl
from jax.experimental.pallas import tpu as pltpu
from jax.sharding import PartitionSpec as P

EDOF = 12
ITERS = 3
SMOOTH = 2
FIBRE_RATE = 0.3
ISO_RATE = 0.05
EPSILON = 1e-06

F32 = jnp.float32
BF16 = jnp.bfloat16
I32 = jnp.int32
MESH = pl.DeviceIdType.MESH
LANES = 128
CHUNK = 256
RP = 16
GROUP = 32
MARGIN_R = 4
MARGIN_C = 64


def iota(shape, dim):
    return lax.broadcasted_iota(I32, shape, dim)


def hot(cond):
    return jnp.where(cond, 1.0, 0.0).astype(BF16)


def split(value):
    high = value.astype(BF16)
    return high, (value - high.astype(F32)).astype(BF16)


def kernel(
    ns, nl,
    a_h, rhs_h, par_h, b_h, ci_h, damp_h, rec_h, base_h, adj_h, ev_h, fc_h,
    x_o, f_o,
    a, rhs, par, b, ci, damp, rec, base, adj, evb, fcb,
    own_hot, recv_hot, send_hot, x, xb, img, tmp, res, parts, snd, rcv,
    bwide, bt, bp, spread, cpf, cp, ag, ck, prod, sel, egb, colhot, rowhot, rowval,
    lsem, nsend, nrecv, gsend, grecv, vsend, vrecv, csend, crecv, esend, erecv,
):
    n = ns * nl
    spots = a.shape[0]
    quarter = spots // 4
    modes = b.shape[0]
    sub, load = lax.axis_index("sub"), lax.axis_index("load")
    me = sub * nl + load

    def dev(p):
        return (lax.div(p, nl), lax.rem(p, nl))

    def peer(k):
        return lax.rem(me + k, n)

    local = [
        pltpu.make_async_copy(src, dst, lsem.at[i])
        for i, (src, dst) in enumerate((
            (par_h, par),
            (b_h.at[0], b),
            (ci_h, ci),
            (ev_h, evb.at[me]),
            (fc_h, fcb.at[4]),
            (damp_h, damp),
            (a_h.at[0], a),
            (rhs_h.at[0], rhs),
            (rec_h.at[0], rec),
            (base_h.at[0], base),
            (adj_h.at[0], adj),
        ))
    ]
    for i in (1, 7, 0, 2, 5, 6, 3, 4):
        local[i].start()

    barrier = pltpu.get_barrier_semaphore()

    def each_peer(act):
        @pl.loop(0, ns)
        def _(i):
            far = jnp.where(2 * sub < ns, ns - 1 - i, i)
            for j in range(nl):
                across = jnp.where(2 * load < nl, nl - 1 - j, j)

                @pl.when(far * nl + across != me)
                def _():
                    act((far, across))

    each_peer(lambda to: pl.semaphore_signal(barrier, inc=1, device_id=to, device_id_type=MESH))

    def to_all(ref, send, recv):
        each_peer(lambda to: pltpu.make_async_remote_copy(
            src_ref=ref.at[me], dst_ref=ref.at[me], send_sem=send, recv_sem=recv,
            device_id=to, device_id_type=MESH,
        ).start())

    def settle(ref, sem):
        part = ref.at[pl.ds(0, n - 1)]
        pltpu.make_async_copy(part, part, sem).wait()

    blocks = spots // LANES
    local[1].wait()
    bwide[...] = jnp.zeros_like(bwide)
    basis = b[...].astype(F32)
    bwide[0:modes, :] = basis
    bwide[RP:RP + modes, :] = basis
    bp[...] = bwide[0:RP, :].astype(BF16)
    local[7].wait()

    def keep_parts(rows, left, total):
        res[rows, :] = left
        high, rest = split(left)
        parts[rows, 0:LANES] = high
        parts[rows, LANES:2 * LANES] = rest
        return total + jnp.sum((left * left).reshape(CHUNK // 8, 8, LANES), axis=0)

    def send_terms(it, total):
        both = jnp.dot(bp[...], parts[...], preferred_element_type=F32)
        terms = both[:, 0:LANES] + both[:, LANES:2 * LANES]
        squares = jnp.sum(total, axis=0, keepdims=True)
        high, rest = split(squares)
        row = iota((RP, LANES), 0)
        terms = jnp.where(row == modes, high.astype(F32), terms)
        terms = jnp.where(row == modes + 1, rest.astype(F32), terms)
        ag[it, me] = terms.astype(BF16)
        if it == 0:
            pl.semaphore_wait(barrier, n - 1)
        to_all(ag.at[it], gsend.at[it], grecv.at[it])

    entries = float(n * spots)
    near = []
    for it in range(ITERS):
        total = jnp.zeros((8, LANES), F32)
        if it == 0:
            for r in range(spots // CHUNK):
                rows = pl.ds(r * CHUNK, CHUNK)
                total = keep_parts(rows, rhs[rows, :], total)
            send_terms(it, total)
        else:
            for r in range(spots // CHUNK):
                rows = pl.ds(r * CHUNK, CHUNK)
                img[rows, :] = jnp.dot(a[rows, :], xb[...], preferred_element_type=F32).astype(BF16)
            for side, step in enumerate((1, n - 1)):
                half = pl.ds(side * quarter, quarter)
                snd[it, half] = jnp.dot(
                    send_hot[half, :], img[...], preferred_element_type=F32
                ).astype(BF16)
                copy = pltpu.make_async_remote_copy(
                    src_ref=snd.at[it, half], dst_ref=rcv.at[it, half],
                    send_sem=nsend.at[it, side], recv_sem=nrecv.at[it, side],
                    device_id=dev(peer(step)), device_id_type=MESH,
                )
                copy.start()
                near.append(copy)
            for r in range(spots // CHUNK):
                rows = pl.ds(r * CHUNK, CHUNK)
                tmp[rows, :] = rhs[rows, :] - (img[rows, :].astype(F32) + jnp.dot(
                    own_hot[rows, :], img[...], preferred_element_type=F32
                ))
            near[-2].wait_recv()
            near[-1].wait_recv()
            for r in range(spots // CHUNK):
                rows = pl.ds(r * CHUNK, CHUNK)
                left = tmp[rows, :] - jnp.dot(
                    recv_hot[rows, :], rcv[it], preferred_element_type=F32
                )
                total = keep_parts(rows, left, total)
            send_terms(it, total)

        if it == 0:
            local[3].wait()
            local[4].wait()
            local[5].wait()
            local[6].wait()
            for copy in local[8:]:
                copy.start()
        if it == 0:
            to_all(evb, vsend, vrecv)
            around = [(i, j) for i in (-1, 0, 1) for j in (-1, 0, 1) if (i, j) != (0, 0)]
            for i, j in around:
                pltpu.make_async_remote_copy(
                    src_ref=fcb.at[4], dst_ref=fcb.at[(1 - i) * 3 + 1 - j],
                    send_sem=csend, recv_sem=crecv,
                    device_id=(lax.rem(sub + i + ns, ns), lax.rem(load + j + nl, nl)),
                    device_id_type=MESH,
                ).start()
        if it == 0:
            for r in range(blocks):
                bt[pl.ds(r * LANES, LANES), :] = jnp.transpose(
                    bwide[:, r * LANES:(r + 1) * LANES]
                ).astype(BF16)
            ck[...] = jnp.zeros_like(ck)
            local[2].wait()
            deep, broad = spread.shape
            at_col = iota((deep, broad), 1)
            within = at_col & (RP - 1)
            from_row = (at_col >> 4) * modes + within
            spread[...] = hot((iota((deep, broad), 0) == from_row) & (within < modes))
            cpf[...] = jnp.zeros_like(cpf)
            for g in range(n // GROUP):
                high, rest = split(ci[:, g * deep:(g + 1) * deep])
                cols = pl.ds(g * broad, broad)
                cpf[0:modes, cols] = jnp.dot(high, spread[...], preferred_element_type=F32)
                cpf[RP:RP + modes, cols] = jnp.dot(rest, spread[...], preferred_element_type=F32)
                mode = iota((1, broad), 1) & (RP - 1)
                cpf[modes:modes + 1, cols] = jnp.where((mode == modes) | (mode == modes + 1), 1.0, 0.0)
            cp[...] = cpf[...].astype(BF16)
            offset = iota(sel.shape, 1) - EDOF * iota(sel.shape, 0)
            sel[...] = hot((offset >= 0) & (offset < EDOF))

            local[0].wait()
            prow = par[...].astype(F32)
            lane = iota((LANES, LANES), 1).astype(F32)
            for r in range(blocks):
                rows = pl.ds(r * LANES, LANES)
                pcol = jnp.transpose(jnp.broadcast_to(prow[:, r * LANES:(r + 1) * LANES], (LANES, LANES)))
                below = jnp.zeros((LANES, LANES), F32)
                for c in range(blocks):
                    cols = pl.ds(c * LANES, LANES)
                    own_hot[rows, cols] = hot(pcol == lane + float(spots + c * LANES))
                    below = below + jnp.where(pcol > prow[:, c * LANES:(c + 1) * LANES], 1.0, 0.0)
                rank = jnp.broadcast_to(jnp.sum(below, axis=1, keepdims=True), (LANES, LANES))
                place = jnp.where(
                    pcol < float(spots),
                    rank,
                    jnp.where(pcol >= float(2 * spots), rank - float(2 * quarter), -1.0),
                )
                for c in range(2 * quarter // LANES):
                    recv_hot[rows, pl.ds(c * LANES, LANES)] = hot(place == lane + float(c * LANES))
            to_next = jnp.where(prow >= float(2 * spots), 1.0, 0.0)
            to_prev = jnp.where(prow < float(spots), 1.0, 0.0)
            count = jnp.where(iota((8, spots), 0) == 0, to_next, to_prev)
            wide = iota((8, spots), 1)
            shift = 1
            while shift < spots:
                count = count + jnp.where(wide >= shift, pltpu.roll(count, shift, 1), 0.0)
                shift *= 2
            slot = jnp.where(
                to_next > 0.5,
                count[0:1] - 1.0,
                jnp.where(to_prev > 0.5, count[1:2] - 1.0 + float(quarter), -1.0),
            )
            for r in range(2 * quarter // LANES):
                at = (iota((LANES, spots), 0) + r * LANES).astype(F32)
                send_hot[pl.ds(r * LANES, LANES), :] = hot(slot == at)

        if it == 1:
            settle(evb, vrecv)

            @pl.loop(0, n)
            def _(s):
                column = evb[s] & (LANES - 1)
                spot = (lax.rem(s, nl) - load) * LANES + column + MARGIN_C
                cols = pl.ds(pl.multiple_of(s * LANES, LANES), LANES)
                spots_at = jnp.transpose(jnp.broadcast_to(spot.astype(F32), (LANES, LANES)))
                here = iota((LANES, LANES), 1).astype(F32)
                colhot[cols, 0:LANES] = hot(spots_at == here)
                colhot[cols, LANES:2 * LANES] = hot(spots_at == here + float(LANES))
                rowhot[:, cols] = hot(iota((RP, LANES), 0) == (evb[s] >> 7) - (sub * 8 - MARGIN_R))

        settle(ag.at[it], grecv.at[it])
        solved = jnp.dot(
            cp[...], ag[it].reshape(n * RP, LANES), preferred_element_type=F32
        )
        correction = solved[0:RP] + solved[RP:2 * RP]
        mean = correction[modes:modes + 1] / entries
        step_size = damp[...] / jnp.sqrt(mean + EPSILON)
        high, rest = split(correction)
        ck[0:RP, :] = high
        ck[RP:2 * RP, :] = rest

        @pl.loop(0, spots // CHUNK, unroll=True)
        def _(r):
            rows = pl.ds(pl.multiple_of(r * CHUNK, CHUNK), CHUNK)
            projected = res[rows, :] - jnp.dot(bt[rows, :], ck[...], preferred_element_type=F32)
            new = step_size * projected if it == 0 else x[rows, :] + step_size * projected
            if it == ITERS - 1:
                x_o[0, rows, :] = new
            else:
                x[rows, :] = new
            xb[rows, :] = new.astype(BF16)

    for copy in local[8:]:
        copy.wait()
    unknowns = rec.shape[0]

    @pl.loop(0, unknowns // CHUNK, unroll=True)
    def _(r):
        rows = pl.ds(pl.multiple_of(r * CHUNK, CHUNK), CHUNK)
        displaced = base[rows, :].astype(F32) - jnp.dot(
            rec[rows, :], xb[...], preferred_element_type=F32
        )
        high, rest = split(displaced * adj[rows, :].astype(F32))
        prod[rows, 0:LANES] = high
        prod[rows, LANES:2 * LANES] = rest

    both = jnp.dot(sel[...], prod[...], preferred_element_type=F32)
    grads = jnp.sum(
        jnp.transpose(both[:, 0:LANES] + both[:, LANES:2 * LANES]), axis=0, keepdims=True
    ) / math.sqrt(EDOF * LANES)
    egb[me] = grads
    to_all(egb, esend, erecv)

    pltpu.make_async_copy(fcb.at[pl.ds(0, 8)], fcb.at[pl.ds(0, 8)], crecv).wait()
    classes = jnp.concatenate(
        [jnp.concatenate([fcb[3 * i + j] for j in range(3)], axis=1) for i in range(3)], axis=0
    )
    high_r, wide_c = 2 * 8, 2 * LANES
    classes = pltpu.roll(classes, 3 * 8 - (8 - MARGIN_R), 0)[0:high_r]
    classes = pltpu.roll(classes, 3 * LANES - (LANES - MARGIN_C), 1)[:, 0:wide_c]
    grid_row = iota((high_r, wide_c), 0) + (sub * 8 - MARGIN_R)
    grid_col = iota((high_r, wide_c), 1) + (load * LANES - MARGIN_C)
    inside = (grid_row >= 0) & (grid_row < ns * 8) & (grid_col >= 0) & (grid_col < nl * LANES)

    settle(egb, erecv)

    def place_rows(s, carry):
        cols = pl.ds(pl.multiple_of(s * LANES, LANES), LANES)
        here = rowhot[:, cols]
        high, rest = split(jnp.broadcast_to(egb[s], (RP, LANES)))
        rowval[0:RP, cols] = high * here
        rowval[RP:2 * RP, cols] = rest * here
        return carry

    lax.fori_loop(0, n, place_rows, 0, unroll=min(n, 32))
    sums = jnp.dot(rowval[...], colhot[...], preferred_element_type=F32)
    field = sums[0:RP] + sums[RP:2 * RP]

    def moved(value, by_row, by_col):
        if by_row:
            value = pltpu.roll(value, (-by_row) % high_r, 0)
        if by_col:
            value = pltpu.roll(value, (-by_col) % wide_c, 1)
        return value

    for repeat in range(SMOOTH):
        field = jnp.where(inside, field, 0.0)
        up, down = moved(field, 1, 0), moved(field, -1, 0)
        along_rows = up + down - 2.0 * field
        along_cols = moved(field, 0, 1) + moved(field, 0, -1) - 2.0 * field
        diag_main = moved(up, 0, 1) + moved(down, 0, -1) - 2.0 * field
        diag_anti = moved(up, 0, -1) + moved(down, 0, 1) - 2.0 * field
        chosen = jnp.where(
            classes == 0,
            along_rows,
            jnp.where(classes == 1, along_cols, jnp.where(classes == 2, diag_main, diag_anti)),
        )
        field = field + FIBRE_RATE * chosen + ISO_RATE * (along_rows + along_cols)
    f_o[...] = moved(field, MARGIN_R, MARGIN_C)[0:8, 0:LANES]

    for copy in near:
        copy.wait_send()
    for it in range(ITERS):
        settle(ag.at[it], gsend.at[it])
    settle(evb, vsend)
    settle(egb, esend)
    pltpu.make_async_copy(fcb.at[pl.ds(0, 8)], fcb.at[pl.ds(0, 8)], csend).wait()


def deliver(x, field, x_h, f_h, sem):
    copies = [
        pltpu.make_async_copy(x, x_h, sem.at[0]),
        pltpu.make_async_copy(field, f_h, sem.at[1]),
    ]
    for copy in copies:
        copy.start()
    for copy in copies:
        copy.wait()


def on_device(ns, nl, *args):
    (dual_ops, dual_rhs, partner, coarse_basis, coarse_inverse, damping,
     recovery, base_disp, adjoint, elem_voxel, fibre_class) = args
    n = ns * nl
    spots, columns = dual_rhs.shape[1:]
    modes = coarse_basis.shape[1]
    unknowns = recovery.shape[1]
    elements = elem_voxel.shape[1]
    half = spots // 2
    dma = pltpu.SemaphoreType.DMA
    scratch = [
        pltpu.VMEM((spots, spots), BF16),
        pltpu.VMEM((spots, columns), F32),
        pltpu.VMEM((1, spots), I32),
        pltpu.VMEM((modes, spots), BF16),
        pltpu.VMEM(coarse_inverse.shape, F32),
        pltpu.VMEM((1, columns), F32),
        pltpu.VMEM((unknowns, spots), BF16),
        pltpu.VMEM((unknowns, columns), BF16),
        pltpu.VMEM((unknowns, columns), BF16),
        pltpu.VMEM((n, 1, elements), I32),
        pltpu.VMEM((9,) + fibre_class.shape, I32),
        pltpu.VMEM((spots, spots), BF16),
        pltpu.VMEM((spots, half), BF16),
        pltpu.VMEM((half, spots), BF16),
        pltpu.VMEM((spots, columns), F32),
        pltpu.VMEM((spots, columns), BF16),
        pltpu.VMEM((spots, columns), BF16),
        pltpu.VMEM((spots, columns), F32),
        pltpu.VMEM((spots, columns), F32),
        pltpu.VMEM((spots, 2 * columns), BF16),
        pltpu.VMEM((ITERS, half, columns), BF16),
        pltpu.VMEM((ITERS, half, columns), BF16),
        pltpu.VMEM((LANES, spots), F32),
        pltpu.VMEM((spots, LANES), BF16),
        pltpu.VMEM((RP, spots), BF16),
        pltpu.VMEM((GROUP * modes, GROUP * RP), BF16),
        pltpu.VMEM((2 * RP, n * RP), F32),
        pltpu.VMEM((2 * RP, n * RP), BF16),
        pltpu.VMEM((ITERS, n, RP, columns), BF16),
        pltpu.VMEM((LANES, columns), BF16),
        pltpu.VMEM((unknowns, 2 * columns), BF16),
        pltpu.VMEM((elements, unknowns), BF16),
        pltpu.VMEM((n, 1, elements), F32),
        pltpu.VMEM((n * elements, 2 * LANES), BF16),
        pltpu.VMEM((RP, n * elements), BF16),
        pltpu.VMEM((2 * RP, n * elements), BF16),
        dma((11,)),
        dma((ITERS, 2)),
        dma((ITERS, 2)),
        dma((ITERS,)),
        dma((ITERS,)),
        dma, dma, dma, dma, dma, dma,
    ]
    anywhere = pl.BlockSpec(memory_space=pl.ANY)
    held = pl.BlockSpec(memory_space=pltpu.VMEM)
    multipliers, field = pl.pallas_call(
        functools.partial(kernel, ns, nl),
        out_shape=(
            pltpu.VMEM((1, spots, columns), F32),
            pltpu.VMEM(fibre_class.shape, F32),
        ),
        in_specs=[anywhere] * 11,
        out_specs=(held, held),
        scratch_shapes=scratch,
        compiler_params=pltpu.CompilerParams(
            collective_id=0, has_side_effects=True, vmem_limit_bytes=62 * 1024 * 1024
        ),
    )(
        dual_ops, dual_rhs, partner, coarse_basis, coarse_inverse,
        damping.reshape(1, columns), recovery, base_disp, adjoint, elem_voxel, fibre_class,
    )
    return pl.pallas_call(
        deliver,
        out_shape=(
            jax.ShapeDtypeStruct((1, spots, columns), F32),
            jax.ShapeDtypeStruct(fibre_class.shape, F32),
        ),
        in_specs=[anywhere, anywhere],
        out_specs=(anywhere, anywhere),
        scratch_shapes=[dma((2,))],
    )(pltpu.with_memory_space_constraint(multipliers, pltpu.VMEM), pltpu.with_memory_space_constraint(field, pltpu.VMEM))


def solution(mesh):
    ns, nl = mesh.shape["sub"], mesh.shape["load"]
    placed = (
        P(("sub", "load"), None, None),
        P(("sub", "load"), None, None),
        P(("sub", "load"), None),
        P(("sub", "load"), None, None),
        P(("sub", "load"), None),
        P(),
        P(("sub", "load"), None, None),
        P(("sub", "load"), None, None),
        P(("sub", "load"), None, None),
        P(("sub", "load"), None),
        P("sub", "load"),
    )
    return jax.shard_map(
        functools.partial(on_device, ns, nl),
        mesh=mesh,
        in_specs=placed,
        out_specs=(P(("sub", "load"), None, None), P("sub", "load")),
        check_vma=False,
    )
```
